256 devices in a mesh: ctx: 32 (over z, y_lo, core), head: 8 (over x, y_hi).
Axes of the slice: x: 4, y: 4 (y_hi: 2, y_lo: 2; y = y_hi * 2 + y_lo), z: 8, core: 2. Of those that a mesh axis runs over, the one named last changes fastest.
Arguments:
- queries: bfloat16 [4096, 8192], P('ctx', 'head'), may hold values from -5 to 5
- key_rows: bfloat16 [4096, 1024], P('ctx', 'head'), may hold values from -5 to 5
- value_rows: bfloat16 [4096, 1024], P('ctx', 'head'), may hold values from -6 to 6
- query_tangent: bfloat16 [4096, 8192], P('ctx', 'head'), may hold values from -16 to 16
- key_tangent: bfloat16 [4096, 1024], P('ctx', 'head'), may hold values from -3 to 3
- value_tangent: bfloat16 [4096, 1024], P('ctx', 'head'), may hold values from -6 to 6
- block_order: int32 [32], replicated, may hold values from 0 to 31, each once
Outputs:
- attended: bfloat16 [4096, 8192], P('ctx', 'head')
- probe_out: bfloat16 [4096, 8192], P('ctx', 'head')
- probe_norm: float32 [], replicated
The draws below stay inside these ranges and needn't reach their ends.
Inputs may be any that keep to these rules, and one draw needn't show every extreme that they name: `block_order`: each block index appears exactly once.
All inputs are finite; a program needn't handle non-finite values.
Results may differ from the reference program's by a relative error of at most 0.025.
Values may be sent and summed in bfloat16 or wider, within the bound.
No kernel may reach another device: no remote copies, remote signals or barrier semaphores. Data moves between devices by JAX's collectives and lax.ppermute only.
A program may use at most 64 MiB of HBM per device.

```python
import math
import jax
import jax.numpy as jnp
from jax import lax

Q_HEADS = 64
KV_HEADS = 8
HEAD_DIM = 128
TOK_DEV = 128
SEQUENCE = 4096
N_CTX = 32


def paired_rows(key):
    base = jax.random.fold_in(key, 11)
    key_q, key_k = jax.random.split(base, 2)
    width_q = Q_HEADS * HEAD_DIM
    width_k = KV_HEADS * HEAD_DIM
    query_part = jnp.clip(1.6 * jax.random.normal(key_q, (SEQUENCE, width_q)), -5.0, 5.0)
    key_part = jnp.clip(1.6 * jax.random.normal(key_k, (SEQUENCE, width_k)), -5.0, 5.0)
    return (query_part, key_part)


def draw_queries(key, part):
    query_part, key_part = paired_rows(key)
    return query_part.astype(jnp.bfloat16)


def draw_key_rows(key, part):
    query_part, key_part = paired_rows(key)
    return key_part.astype(jnp.bfloat16)


def draw_query_tangent(key, part):
    base = jax.random.fold_in(key, 23)
    key_raw, key_spread = jax.random.split(base, 2)
    width_q = Q_HEADS * HEAD_DIM
    fraction = jnp.arange(SEQUENCE, dtype=jnp.float32) / max(SEQUENCE - 1, 1)
    spread = jax.random.uniform(key_spread, (SEQUENCE,))
    row_scale = 10.0 ** (0.5 * fraction + 0.5 * spread)
    raw = jnp.clip(0.4 * jax.random.normal(key_raw, (SEQUENCE, width_q)), -1.6, 1.6)
    return (raw * row_scale[:, None]).astype(jnp.bfloat16)


def block_scale(key, dims, cuts, smallest, high):
    def one(dim, shards_of):
        heights = jax.random.uniform(jax.random.fold_in(jax.random.fold_in(key, 6), dim), (shards_of,), jnp.float32, smallest / len(cuts), high / len(cuts))
        return jnp.repeat(jnp.exp(heights), dims[dim] // shards_of).reshape((-1,) + (1,) * (len(dims) - dim - 1))

    loudness = one(*cuts[0])
    for cut in cuts[1:]:
        loudness = loudness * one(*cut)
    return loudness


def bell_draw(key, dims, deviation, reach, pieces=(), kind=jnp.bfloat16):
    values = jax.random.normal(key, dims, jnp.float32) * deviation
    if len(pieces) > 0:
        values = block_scale(key, dims, pieces, -0.22, 0.18) * values
    return jnp.clip(values, min=-reach, max=reach).astype(kind)


def setup_inputs(seed: int = 0) -> dict:
    key_list = jax.random.split(jax.random.key(seed), 8)
    return {
        "queries": draw_queries(jax.random.fold_in(key_list[7], 71), 0),
        "key_rows": draw_key_rows(jax.random.fold_in(key_list[7], 71), 0),
        "value_rows": bell_draw(key_list[2], (SEQUENCE, KV_HEADS * HEAD_DIM), 1.0, 6.0, ((0, 32), (1, 8))),
        "query_tangent": draw_query_tangent(jax.random.fold_in(key_list[7], 71), 0),
        "key_tangent": bell_draw(key_list[4], (SEQUENCE, KV_HEADS * HEAD_DIM), 0.5, 3.0, ((0, 32), (1, 8))),
        "value_tangent": bell_draw(key_list[5], (SEQUENCE, KV_HEADS * HEAD_DIM), 1.0, 6.0, ((0, 32), (1, 8))),
        "block_order": jax.random.permutation(key_list[6], N_CTX).astype(jnp.int32),
    }


floor_score = -1e+30

def reference(queries, key_rows, value_rows, query_tangent, key_tangent, value_tangent, block_order):
    row_index = jnp.arange(SEQUENCE, dtype=jnp.int32)
    position = block_order[row_index // TOK_DEV].astype(jnp.int32) * TOK_DEV + row_index % TOK_DEV
    visible = position[None, :] <= position[:, None]
    shares = Q_HEADS // KV_HEADS
    factor = 1.0 / math.sqrt(HEAD_DIM)

    def per_head(head):
        group = head // shares
        q_head = lax.dynamic_slice_in_dim(queries, head * HEAD_DIM, HEAD_DIM, 1)
        dq_head = lax.dynamic_slice_in_dim(query_tangent, head * HEAD_DIM, HEAD_DIM, 1)
        k_head = lax.dynamic_slice_in_dim(key_rows, group * HEAD_DIM, HEAD_DIM, 1)
        dk_head = lax.dynamic_slice_in_dim(key_tangent, group * HEAD_DIM, HEAD_DIM, 1)
        v_head = lax.dynamic_slice_in_dim(value_rows, group * HEAD_DIM, HEAD_DIM, 1)
        dv_head = lax.dynamic_slice_in_dim(value_tangent, group * HEAD_DIM, HEAD_DIM, 1)
        scores = jnp.dot(q_head, k_head.T, preferred_element_type=jnp.float32) * factor
        masked = jnp.where(visible, scores, floor_score)
        top = lax.optimization_barrier(jnp.max(masked, axis=1, keepdims=True))
        weights = jnp.where(visible, jnp.exp(masked - top), 0.0)
        totals = lax.optimization_barrier(jnp.sum(weights, axis=1, keepdims=True))
        slopes = (jnp.dot(dq_head, k_head.T, preferred_element_type=jnp.float32) + jnp.dot(q_head, dk_head.T, preferred_element_type=jnp.float32)) * factor
        tilted = weights * slopes
        drifts = lax.optimization_barrier(jnp.sum(tilted, axis=1, keepdims=True))
        low_weights = weights.astype(jnp.bfloat16)
        low_tilted = tilted.astype(jnp.bfloat16)
        numerator = jnp.dot(low_weights, v_head, preferred_element_type=jnp.float32)
        tangent_num = jnp.dot(low_tilted, v_head, preferred_element_type=jnp.float32) + jnp.dot(low_weights, dv_head, preferred_element_type=jnp.float32)
        attended = (numerator / totals).astype(jnp.bfloat16)
        probe = (tangent_num - numerator * drifts / totals) / totals
        return (attended, probe)
    heads_out, probes = lax.map(per_head, jnp.arange(Q_HEADS, dtype=jnp.int32))
    attended = heads_out.transpose(1, 0, 2).reshape(SEQUENCE, Q_HEADS * HEAD_DIM)
    probe_all = probes.transpose(1, 0, 2).reshape(SEQUENCE, Q_HEADS * HEAD_DIM)
    probe_norm = jnp.sqrt(jnp.sum(probe_all * probe_all) / (SEQUENCE * Q_HEADS * HEAD_DIM))
    return (attended, probe_all.astype(jnp.bfloat16), probe_norm)
```

```python
import functools
import math

import jax
import jax.numpy as jnp
from jax import lax
from jax.experimental import pallas as pl
from jax.experimental.pallas import tpu as pltpu
from jax.sharding import PartitionSpec as P

T = 128
D = 128
H = 8
NEG = -1e30
FACTOR = 1.0 / math.sqrt(D)
EXP2_FACTOR = math.log2(math.e) / math.sqrt(D)
LAST = (((1,), (1,)), ((), ()))
VMEM = pltpu.VMEM


def at(z, y, c):
    return (z % 8) * 4 + y * 2 + c


PLACES = [(z, y, c) for z in range(8) for y in range(2) for c in range(2)]


def along_z(step):
    return [(at(z, y, c), at(z + (step if c == 0 else -step), y, c)) for z, y, c in PLACES]


ACROSS_Y = [(at(z, y, c), at(z, 1 - y, c)) for z, y, c in PLACES]
ACROSS_CORE = [(at(z, y, c), at(z, y, 1 - c)) for z, y, c in PLACES]


def send_z(piece, step):
    rows, slots = piece
    return lax.ppermute(rows, "ctx", along_z(step)), [(k - step, dy, dc) for k, dy, dc in slots]


def send_y(piece):
    rows, slots = piece
    return lax.ppermute(rows, "ctx", ACROSS_Y), [(k, 1 - dy, dc) for k, dy, dc in slots]


def send_core(piece):
    rows, slots = piece
    return lax.ppermute(rows, "ctx", ACROSS_CORE), [(-k, dy, 1 - dc) for k, dy, dc in slots]


def join(*pieces):
    return (
        jnp.concatenate([p[0] for p in pieces], axis=0),
        [s for p in pieces for s in p[1]],
    )


def head_rows(piece, count):
    return piece[0][: count * T], piece[1][:count]


def stage_kernel(slot_lists, first, last, *refs):
    refs = list(refs)
    order = refs.pop(0)
    q_ref, dq_ref = refs.pop(0), refs.pop(0)
    pieces = [refs.pop(0) for _ in slot_lists]
    if not first:
        old_sums, old_stats = refs.pop(0), refs.pop(0)
    if last:
        out_ref, probe_ref, square_ref = refs
    else:
        new_sums, new_stats = refs
    me = lax.axis_index("ctx")
    z, y, c = me // 4, (me // 2) % 2, me % 2
    way = 1 - 2 * c
    mine = order[me]

    def seen(slot):
        k, dy, dc = slot
        source = ((z + 8 + k * way) % 8) * 4 + ((y + dy) % 2) * 2 + (c + dc) % 2
        return order[source] <= mine

    visible = [[None if s == (0, 0, 0) else seen(s) for s in slots] for slots in slot_lists]
    row = lax.broadcasted_iota(jnp.int32, (T, T), 0)
    col = lax.broadcasted_iota(jnp.int32, (T, T), 1)
    lower = col <= row
    squares = jnp.zeros((T, D), jnp.float32)
    for h in range(H):
        columns = pl.ds(h * D, D)
        q = q_ref[:, columns]
        dq_q = jnp.concatenate([dq_ref[:, columns], q], axis=1)
        scores = []
        for piece, flags in zip(pieces, visible):
            s = lax.dot_general(q, piece[:, :D], LAST, preferred_element_type=jnp.float32)
            parts = []
            for b, flag in enumerate(flags):
                part = s[:, b * T : (b + 1) * T]
                parts.append(jnp.where(lower if flag is None else flag, part, NEG))
            scores.append(parts)
        top = functools.reduce(jnp.maximum, [p for parts in scores for p in parts])
        top = jnp.max(top, axis=1, keepdims=True)
        if not first:
            stats = old_stats[h * T : (h + 1) * T, :]
            old_top = stats[:, 0:1]
            top = jnp.maximum(top, old_top)
            shrink = jnp.exp2((old_top - top) * EXP2_FACTOR)
        total = drift = tangent = sums = None
        for piece, parts in zip(pieces, scores):
            slope = lax.dot_general(
                dq_q, piece[:, : 2 * D], LAST, preferred_element_type=jnp.float32
            )
            weights, tilts = [], []
            for b, part in enumerate(parts):
                w = jnp.exp2((part - top) * EXP2_FACTOR)
                t = w * slope[:, b * T : (b + 1) * T]
                total = w if total is None else total + w
                drift = t if drift is None else drift + t
                weights.append(w.astype(jnp.bfloat16))
                tilts.append(t.astype(jnp.bfloat16))
            w = jnp.concatenate(weights, axis=1)
            t = jnp.concatenate(tilts, axis=1)
            a = jnp.dot(w, piece[:, 2 * D :], preferred_element_type=jnp.float32)
            b = jnp.dot(t, piece[:, 2 * D : 3 * D], preferred_element_type=jnp.float32)
            sums = a if sums is None else sums + a
            tangent = b if tangent is None else tangent + b
        total = jnp.sum(total, axis=1, keepdims=True)
        drift = jnp.sum(drift, axis=1, keepdims=True) * FACTOR
        numer = sums[:, :D]
        tangent = sums[:, D:] + tangent * FACTOR
        if not first:
            total = total + shrink * stats[:, 1:2]
            drift = drift + shrink * stats[:, 2:3]
            old = old_sums[h * T : (h + 1) * T, :]
            numer = numer + shrink * old[:, :D]
            tangent = tangent + shrink * old[:, D:]
        if last:
            inverse = 1.0 / total
            attended = numer * inverse
            probe = (tangent - attended * drift) * inverse
            out_ref[:, columns] = attended.astype(jnp.bfloat16)
            probe_ref[:, columns] = probe.astype(jnp.bfloat16)
            squares = squares + probe * probe
        else:
            new_sums[h * T : (h + 1) * T, :D] = numer
            new_sums[h * T : (h + 1) * T, D:] = tangent
            new_stats[h * T : (h + 1) * T, :] = jnp.where(
                col == 0, top, jnp.where(col == 1, total, drift)
            )
    if last:
        lanes = jnp.sum(squares, axis=0, keepdims=True)
        square_ref[...] = jnp.broadcast_to(lanes, square_ref.shape)


def stage(order, q, dq, pieces, state, last, devices):
    first = state is None
    slots = [p[1] for p in pieces]
    operands = [order, q, dq] + [p[0] for p in pieces] + ([] if first else list(state))
    rows = H * T
    if last:
        shapes = [(T, H * D, jnp.bfloat16), (T, H * D, jnp.bfloat16), (devices, D, jnp.float32)]
    else:
        shapes = [(rows, 2 * D, jnp.float32), (rows, D, jnp.float32)]
    blocks = sum(len(s) for s in slots)
    keys = blocks * T
    return pl.pallas_call(
        functools.partial(stage_kernel, slots, first, last),
        out_shape=[jax.ShapeDtypeStruct(s[:2], s[2]) for s in shapes],
        in_specs=[pl.BlockSpec(memory_space=pltpu.SMEM)]
        + [pl.BlockSpec(memory_space=VMEM)] * (len(operands) - 1),
        out_specs=[pl.BlockSpec(memory_space=VMEM)] * len(shapes),
        compiler_params=pltpu.CompilerParams(vmem_limit_bytes=32 * 2**20),
        cost_estimate=pl.CostEstimate(
            flops=8 * rows * keys * 2 * D, bytes_accessed=keys * 8 * D, transcendentals=rows * keys
        ),
    )(*operands)


def shards(queries, key_rows, value_rows, query_tangent, key_tangent, value_tangent, block_order):
    devices = lax.axis_size("ctx") * lax.axis_size("head")
    own = (jnp.concatenate([key_rows, key_tangent, value_rows, value_tangent], axis=1), [(0, 0, 0)])
    own_y = send_y(own)
    pair = join(own, send_core(own))
    z1 = send_z(pair, 1)
    z3 = send_z(pair, 3)
    y1 = send_y(z1)
    z24 = send_z(join(z1, head_rows(z3, 1)), 1)
    y3 = send_y(z3)
    y24 = send_z(join(y1, head_rows(y3, 1)), 1)
    c1 = send_core(join(own_y, z1))
    c2 = send_core(join(z3, y1))
    c3 = send_core(join(z24, y3))
    c4 = send_core(y24)
    attended, probe, squares = stage(
        block_order,
        queries,
        query_tangent,
        [pair, own_y, z1, c1, z3, y1, c2, z24, y3, c3, y24, c4],
        None,
        True,
        devices,
    )
    squares = lax.all_to_all(
        squares.reshape(devices, 1, D), ("ctx", "head"), 0, 0, tiled=False
    )
    entries = queries.shape[0] * queries.shape[1] * devices
    probe_norm = jnp.sqrt(jnp.sum(squares) / entries)
    return attended, probe, probe_norm


def solution(mesh):
    sharded = P("ctx", "head")
    return jax.shard_map(
        shards,
        mesh=mesh,
        in_specs=(sharded,) * 6 + (P(),),
        out_specs=(sharded, sharded, P()),
        check_vma=False,
    )
```
